32 devices in a mesh: groups: 2 (over x), tm: 4 (over y, core), chan: 4 (over z).
Axes of the slice: x: 2, y: 2, z: 4, core: 2. Of those that a mesh axis runs over, the one named last changes fastest.
Arguments:
- records: bfloat16 [1536, 1024], P(('groups', 'tm'), 'chan'), parts along dimension 0, may hold values from -6 to 6
- cotangent: bfloat16 [1536, 1024], P(('groups', 'tm'), 'chan'), parts along dimension 0, may hold values from -6 to 6
- filter_weight: bfloat16 [4, 2, 1024, 1024], P(None, None, 'tm', 'chan'), may hold values from -0.125 to 0.125
- gate_weight: bfloat16 [4, 2, 1024, 1024], P(None, None, 'tm', 'chan'), may hold values from -0.125 to 0.125
- mix_weight: bfloat16 [4, 1024, 1024], P(None, 'chan', 'tm'), may hold values from -0.1875 to 0.1875
Outputs:
- output: bfloat16 [1536, 1024], P(('groups', 'tm'), 'chan'), parts along dimension 0
- input_grad: bfloat16 [1536, 1024], P(('groups', 'tm'), 'chan'), parts along dimension 0
The draws below stay inside these ranges and needn't reach their ends.
There are 2 independent parts, one for each index of `groups`. The reference program is written for one: setup_inputs(seed, part) draws one part's arguments, and reference() takes and returns one part's arrays. A program takes and returns all parts, laid end to end along the dimension named above; an argument that names none is the same for every part. Nothing has to cross between parts.
All inputs are finite; a program needn't handle non-finite values.
Results may differ from the reference program's by a relative error of at most 0.018.
Values may be sent and summed in bfloat16 or wider, within the bound.
A program may use at most 64 MiB of HBM per device.

```python
import jax
import jax.numpy as jnp

C = 1024
LAYERS = 4
T_DEV = 192
TIME = 768


def block_levels(stream_key, dims, cuts, least, largest):
    factor_of, own = 1.0, jax.random.fold_in(stream_key, 6)
    for dim, parts in cuts:
        steps = jnp.exp(jax.random.uniform(jax.random.fold_in(own, dim), (parts,), jnp.float32, least / len(cuts), largest / len(cuts)))
        factor_of = factor_of * jnp.repeat(steps, dims[dim] // parts).reshape([-1 if axis == dim else 1 for axis in range(len(dims))])
    return factor_of


def noise(rng, shape, spread, reach, shards=(), held_as=jnp.bfloat16):
    factor_of = block_levels(rng, shape, shards, -0.22, 0.18) if shards else 1.0
    drawn = jax.random.normal(rng, shape, jnp.float32) * spread * factor_of
    return jnp.minimum(jnp.maximum(drawn, -reach), reach).astype(held_as)


def setup_inputs(seed: int = 0, part: int = 0) -> dict:
    splits = jax.random.split(jax.random.key(seed), 6)
    own_keys = jax.random.split(jax.random.fold_in(splits[5], part), 6)
    records = noise(own_keys[0], (TIME, C), 1.0, 6.0, ((0, 4), (1, 4)))
    cotangent = noise(own_keys[1], (TIME, C), 1.0, 6.0, ((0, 4), (1, 4)))
    filter_weight = noise(splits[2], (LAYERS, 2, C, C), (2 * C) ** -0.5, 0.125, ((2, 4), (3, 4)))
    gate_weight = noise(splits[3], (LAYERS, 2, C, C), (2 * C) ** -0.5, 0.125, ((2, 4), (3, 4)))
    mix_weight = noise(splits[4], (LAYERS, C, C), C ** -0.5, 0.1875, ((1, 4), (2, 4)))
    return {"records": records, "cotangent": cotangent, "filter_weight": filter_weight, "gate_weight": gate_weight, "mix_weight": mix_weight}


def delay_rows(values, span):
    count = values.shape[0]
    if span >= count:
        return jnp.zeros_like(values)
    head = jnp.zeros((span, values.shape[1]), values.dtype)
    return jnp.concatenate([head, values[:count - span]], axis=0)


def advance_rows(values, span):
    count = values.shape[0]
    if span >= count:
        return jnp.zeros_like(values)
    tail = jnp.zeros((span, values.shape[1]), values.dtype)
    return jnp.concatenate([values[span:], tail], axis=0)


def reference(records, cotangent, filter_weight, gate_weight, mix_weight):
    signal = records
    stored = []
    for layer_index in range(LAYERS):
        span_rows = T_DEV * 2 ** layer_index
        delayed = delay_rows(signal, span_rows)
        pre_filter = jnp.dot(delayed, filter_weight[layer_index, 0], preferred_element_type=jnp.float32) + jnp.dot(signal, filter_weight[layer_index, 1], preferred_element_type=jnp.float32)
        pre_gate = jnp.dot(delayed, gate_weight[layer_index, 0], preferred_element_type=jnp.float32) + jnp.dot(signal, gate_weight[layer_index, 1], preferred_element_type=jnp.float32)
        gated = (jnp.tanh(pre_filter) * jax.nn.sigmoid(pre_gate)).astype(jnp.bfloat16)
        mix_term = jnp.dot(gated, mix_weight[layer_index], preferred_element_type=jnp.float32)
        signal = (signal.astype(jnp.float32) + mix_term).astype(jnp.bfloat16)
        stored.append((pre_filter, pre_gate))
    output = signal
    grad_now = cotangent
    for layer_index in reversed(range(LAYERS)):
        span_rows = T_DEV * 2 ** layer_index
        pre_filter, pre_gate = stored[layer_index]
        grad_z = jnp.dot(grad_now, mix_weight[layer_index].T, preferred_element_type=jnp.float32)
        tanh_value = jnp.tanh(pre_filter)
        sig_value = jax.nn.sigmoid(pre_gate)
        grad_filt = (grad_z * sig_value * (1.0 - tanh_value * tanh_value)).astype(jnp.bfloat16)
        grad_gate = (grad_z * tanh_value * sig_value * (1.0 - sig_value)).astype(jnp.bfloat16)
        near_term = jnp.dot(grad_filt, filter_weight[layer_index, 1].T, preferred_element_type=jnp.float32) + jnp.dot(grad_gate, gate_weight[layer_index, 1].T, preferred_element_type=jnp.float32)
        far_term = jnp.dot(grad_filt, filter_weight[layer_index, 0].T, preferred_element_type=jnp.float32) + jnp.dot(grad_gate, gate_weight[layer_index, 0].T, preferred_element_type=jnp.float32)
        grad_now = (grad_now.astype(jnp.float32) + near_term + advance_rows(far_term, span_rows)).astype(jnp.bfloat16)
    return output, grad_now
```

```python
import functools

import jax
import jax.numpy as jnp
from jax import lax
from jax.experimental import pallas as pl
from jax.experimental.pallas import tpu as pltpu
from jax.sharding import PartitionSpec as P

MESH = pl.DeviceIdType.MESH
DMA = pltpu.SemaphoreType.DMA
BF = jnp.bfloat16
F32 = jnp.float32


def dot(a, b):
    return jnp.dot(a, b, preferred_element_type=F32)


def dot_t(a, b):
    return lax.dot_general(a, b, (((1,), (1,)), ((), ())), preferred_element_type=F32)


def near_first(count):
    order = []
    for step in range(1, count // 2 + 1):
        for offset in (step, count - step):
            if offset not in order and offset < count:
                order.append(offset)
    return order


def kernel(
    layers, tm, chan,
    rec, cot, f_in, g_in, m_in,
    out, gin,
    fw, gw, mw, sig, dly, rsb, rsr, gr, farb, farr, tval, sval, acc_f, acc_g,
    w_send, w_recv, w_fwd, w_own,
    ag_send, ag_recv, d_send, d_recv, rs_send, rs_recv, f_send, f_recv,
):
    m = lax.axis_index("tm")
    c = lax.axis_index("chan")
    ratio = tm // chan
    rows, cb = rec.shape
    ob = mw.shape[-1]
    partner = m + 1 - 2 * lax.rem(m, 2)
    peers = near_first(chan)
    others = list(range(1, tm // 2))

    def peer(r):
        return lax.rem(c + r, chan)

    def mate(q, base=None):
        return lax.rem((m if base is None else base) + 2 * q, tm)

    def span(l):
        return 2**l

    def far(l):
        return span(l) < tm

    def own_block(l, p):
        if p == 2:
            return m_in.at[l]
        w = (f_in, g_in)[p]
        return w.at[l] if far(l) else w.at[l, 1]

    def slot(l, p, s):
        if p == 2:
            return mw.at[l, s]
        w = (fw, gw)[p]
        return w.at[l, :, s] if far(l) else w.at[l, 1, s]

    def w_copy(l, p, s, to, send, own):
        return pltpu.make_async_remote_copy(
            src_ref=own_block(l, p) if own else slot(l, p, s),
            dst_ref=slot(l, p, s),
            send_sem=send,
            recv_sem=w_recv.at[l * 3 + p, s],
            device_id={"tm": to},
            device_id_type=MESH,
        )

    def w_out(l, p, q):
        if q == 0:
            return w_copy(l, p, m, partner, w_send.at[l * 3 + p, 0], True)
        return w_copy(l, p, m, mate(q), w_send.at[l * 3 + p, q], True)

    def w_on(l, p, q):
        return w_copy(l, p, mate(q), partner, w_fwd.at[l * 3 + p, q], False)

    def w_mine(l, p):
        return pltpu.make_async_copy(own_block(l, p), slot(l, p, m), w_own.at[l * 3 + p])

    def w_start(l):
        for p in range(3):
            for q in others + [0]:
                w_out(l, p, q).start()
            w_mine(l, p).start()

    def w_forward(l):
        for p in range(3):
            for q in others:
                w_on(l, p, q).wait_recv()
                w_on(l, p, q).start()

    def w_ready(l, kinds):
        for p in kinds:
            w_mine(l, p).wait()
            w_copy(l, p, partner, partner, w_fwd.at[l * 3 + p, 0], False).wait_recv()
            for q in others:
                s = mate(q, partner)
                w_copy(l, p, s, partner, w_fwd.at[l * 3 + p, 0], False).wait_recv()

    def ag(i, src, buf, l, r, owner):
        return pltpu.make_async_remote_copy(
            src_ref=src,
            dst_ref=buf.at[l, owner],
            send_sem=ag_send.at[i, r],
            recv_sem=ag_recv.at[i, owner],
            device_id={"chan": peer(r)},
            device_id_type=MESH,
        )

    def ag_start(i, src, buf, l):
        for r in reversed(peers):
            ag(i, src, buf, l, r, c).start()

    def ag_wait(i, buf, l, r):
        ag(i, buf.at[l, c], buf, l, r, peer(r)).wait_recv()

    def rs(i, r, owner):
        return pltpu.make_async_remote_copy(
            src_ref=rsb.at[i, r],
            dst_ref=rsr.at[i, owner],
            send_sem=rs_send.at[i, r],
            recv_sem=rs_recv.at[i, owner],
            device_id={"chan": peer(r)},
            device_id_type=MESH,
        )

    def dl(l, j):
        return pltpu.make_async_remote_copy(
            src_ref=sig.at[l, j],
            dst_ref=dly.at[l, j],
            send_sem=d_send.at[l, j],
            recv_sem=d_recv.at[l, j],
            device_id={"tm": lax.rem(m + span(l), tm)},
            device_id_type=MESH,
        )

    def fr(l, j):
        return pltpu.make_async_remote_copy(
            src_ref=farb.at[l, j],
            dst_ref=farr.at[l, j],
            send_sem=f_send.at[l, j],
            recv_sem=f_recv.at[l, j],
            device_id={"tm": lax.rem(m + tm - span(l), tm)},
            device_id_type=MESH,
        )

    def block(w, l, tap, j):
        return w[l, tap, pl.ds(j * ratio, ratio)].reshape(cb, cb)

    barrier = pltpu.get_barrier_semaphore()
    for s in range(1, tm):
        pl.semaphore_signal(barrier, inc=1, device_id={"tm": lax.rem(m + s, tm)}, device_id_type=MESH)
    for s in range(1, chan):
        pl.semaphore_signal(barrier, inc=1, device_id={"chan": peer(s)}, device_id_type=MESH)
    pl.semaphore_wait(barrier, tm - 1 + chan - 1)

    ag_start(0, rec, sig, 0)
    w_start(0)
    sig[0, c] = rec[...]
    gr[layers - 1, c] = cot[...]
    for l in range(1, layers):
        w_start(l)
    ag_start(layers, cot, gr, layers - 1)

    for l in range(layers):
        if l > 0:
            ag_start(l, sig.at[l, c], sig, l)
        if far(l):
            @pl.when(m < tm - span(l))
            def _():
                dl(l, c).start()
                for r in peers:
                    ag_wait(l, sig, l, r)
                    dl(l, peer(r)).start()

            @pl.when(m >= tm - span(l))
            def _():
                for r in peers:
                    ag_wait(l, sig, l, r)
        if l == 0:
            w_forward(0)
            w_ready(0, (0, 1))
        else:
            w_ready(l, (0, 1))
        for r in [0] + peers:
            j = peer(r)
            if r and not far(l):
                ag_wait(l, sig, l, r)
            x = sig[l, j]
            a = dot(x, block(fw, l, 1, j))
            b = dot(x, block(gw, l, 1, j))
            if r == 0:
                acc_f[...] = a
                acc_g[...] = b
            else:
                acc_f[...] += a
                acc_g[...] += b
        if far(l):
            @pl.when(m >= span(l))
            def _():
                for r in [0] + peers:
                    j = peer(r)
                    dl(l, j).wait_recv()
                    x = dly[l, j]
                    acc_f[...] += dot(x, block(fw, l, 0, j))
                    acc_g[...] += dot(x, block(gw, l, 0, j))
        th = jnp.tanh(acc_f[...])
        sg = jax.nn.sigmoid(acc_g[...])
        tval[l] = th
        sval[l] = sg
        gated = (th * sg).astype(BF)
        w_ready(l, (2,))

        def mixed(j):
            parts = [dot(gated, mw[l, j * ratio + i]) for i in range(ratio)]
            return parts[0] if ratio == 1 else jnp.concatenate(parts, axis=1)

        for r in reversed(peers):
            rsb[l, r] = mixed(peer(r)).astype(BF)
            rs(l, r, c).start()
        acc_f[...] = mixed(c) + sig[l, c].astype(F32)
        if l + 1 < layers:
            w_forward(l + 1)
        for r in peers:
            rs(l, r, peer(r)).wait_recv()
            acc_f[...] += rsr[l, peer(r)].astype(F32)
        if l + 1 < layers:
            sig[l + 1, c] = acc_f[...].astype(BF)
        else:
            out[...] = acc_f[...].astype(BF)

    for l in reversed(range(layers)):
        i = 2 * layers - 1 - l
        if l < layers - 1:
            ag_start(i, gr.at[l, c], gr, l)
        for r in [0] + peers:
            j = peer(r)
            if r:
                ag_wait(i, gr, l, r)
            g = gr[l, j]
            for k in range(ratio):
                z = dot_t(g[:, k * ob:(k + 1) * ob], mw[l, j * ratio + k])
                if r == 0 and k == 0:
                    acc_f[...] = z
                else:
                    acc_f[...] += z
        gz = acc_f[...]
        th = tval[l]
        sg = sval[l]
        gf = (gz * sg * (1.0 - th * th)).astype(BF)
        gg = (gz * th * sg * (1.0 - sg)).astype(BF)
        order = list(reversed(peers)) + [0]
        if far(l):
            @pl.when(m >= span(l))
            def _():
                for r in order:
                    j = peer(r)
                    farb[l, j] = (dot_t(gf, block(fw, l, 0, j)) + dot_t(gg, block(gw, l, 0, j))).astype(BF)
                    fr(l, j).start()
        for r in order:
            j = peer(r)
            acc_g[...] = dot_t(gf, block(fw, l, 1, j)) + dot_t(gg, block(gw, l, 1, j))
            if far(l):
                @pl.when(m < tm - span(l))
                def _():
                    fr(l, j).wait_recv()
                    acc_g[...] += farr[l, j].astype(F32)
            if r:
                rsb[i, r] = acc_g[...].astype(BF)
                rs(i, r, c).start()
        acc_f[...] = acc_g[...] + gr[l, c].astype(F32)
        for r in peers:
            rs(i, r, peer(r)).wait_recv()
            acc_f[...] += rsr[i, peer(r)].astype(F32)
        if l > 0:
            gr[l - 1, c] = acc_f[...].astype(BF)
        else:
            gin[...] = acc_f[...].astype(BF)

    for l in range(layers):
        for p in range(3):
            for q in others:
                w_out(l, p, q).wait_send()
                w_on(l, p, q).wait_send()
            w_out(l, p, 0).wait_send()
        if far(l):
            @pl.when(m < tm - span(l))
            def _():
                for j in range(chan):
                    dl(l, j).wait_send()

            @pl.when(m >= span(l))
            def _():
                for j in range(chan):
                    fr(l, j).wait_send()
    for i in range(2 * layers):
        for r in peers:
            ag(i, rec, sig, 0, r, c).wait_send()
            rs(i, r, c).wait_send()


def local(records, cotangent, filter_weight, gate_weight, mix_weight):
    tm, chan = lax.axis_size("tm"), lax.axis_size("chan")
    layers, taps, ib, cb = filter_weight.shape
    ob = mix_weight.shape[2]
    rows = records.shape[0]
    vmem = pl.BlockSpec(memory_space=pltpu.VMEM)
    hbm = pl.BlockSpec(memory_space=pl.ANY)
    weights = pltpu.VMEM((layers, taps, tm, ib, cb), BF)
    per_layer = pltpu.VMEM((layers, chan, rows, cb), BF)
    both = pltpu.VMEM((2 * layers, chan, rows, cb), BF)
    return pl.pallas_call(
        functools.partial(kernel, layers, tm, chan),
        out_shape=[jax.ShapeDtypeStruct(records.shape, BF)] * 2,
        in_specs=[vmem, vmem, hbm, hbm, hbm],
        out_specs=[vmem, vmem],
        scratch_shapes=[
            weights,
            weights,
            pltpu.VMEM((layers, tm, cb, ob), BF),
            per_layer,
            per_layer,
            both,
            both,
            per_layer,
            per_layer,
            per_layer,
            pltpu.VMEM((layers, rows, cb), F32),
            pltpu.VMEM((layers, rows, cb), F32),
            pltpu.VMEM((rows, cb), F32),
            pltpu.VMEM((rows, cb), F32),
            DMA((3 * layers, tm)),
            DMA((3 * layers, tm)),
            DMA((3 * layers, tm)),
            DMA((3 * layers,)),
            DMA((2 * layers, chan)),
            DMA((2 * layers, chan)),
            DMA((layers, chan)),
            DMA((layers, chan)),
            DMA((2 * layers, chan)),
            DMA((2 * layers, chan)),
            DMA((layers, chan)),
            DMA((layers, chan)),
        ],
        compiler_params=pltpu.CompilerParams(
            collective_id=0, has_side_effects=True, vmem_limit_bytes=56 * 2**20
        ),
    )(records, cotangent, filter_weight, gate_weight, mix_weight)


def solution(mesh):
    return jax.shard_map(
        local,
        mesh=mesh,
        in_specs=(
            P(("groups", "tm"), "chan"),
            P(("groups", "tm"), "chan"),
            P(None, None, "tm", "chan"),
            P(None, None, "tm", "chan"),
            P(None, "chan", "tm"),
        ),
        out_specs=(P(("groups", "tm"), "chan"), P(("groups", "tm"), "chan")),
        check_vma=False,
    )
```

```python
import functools

import jax
import jax.numpy as jnp
from jax import lax
from jax.experimental import pallas as pl
from jax.experimental.pallas import tpu as pltpu
from jax.sharding import PartitionSpec as P

MESH = pl.DeviceIdType.MESH
DMA = pltpu.SemaphoreType.DMA
BF = jnp.bfloat16
F32 = jnp.float32
H = 2


def dot(a, b):
    return jnp.dot(a, b, preferred_element_type=F32)


def dot_t(a, b):
    return lax.dot_general(a, b, (((1,), (1,)), ((), ())), preferred_element_type=F32)


def near_first(count):
    order = []
    for step in range(1, count // 2 + 1):
        for offset in (step, count - step):
            if offset not in order and offset < count:
                order.append(offset)
    return order


def kernel(
    layers, tm, chan,
    rec, cot, f_in, g_in, m_in,
    out, gin,
    fw, gw, mw, sig, dly, rsb, rsr, gr, farb, farr, tval, sval, acc_f, acc_g, gf_s, gg_s,
    w_send, w_recv, w_fwd, w_own,
    ag_send, ag_recv, d_send, d_recv, rs_send, rs_recv, f_send, f_recv,
):
    m = lax.axis_index("tm")
    c = lax.axis_index("chan")
    ratio = tm // chan
    rows, cb = rec.shape
    ob = mw.shape[-1]
    half = rows // H
    partner = m + 1 - 2 * lax.rem(m, 2)
    peers = near_first(chan)
    others = list(range(1, tm // 2))

    def peer(r):
        return lax.rem(c + r, chan)

    def mate(q, base=None):
        return lax.rem((m if base is None else base) + 2 * q, tm)

    def span(l):
        return 2**l

    def far(l):
        return span(l) < tm

    def own_block(l, p):
        if p == 2:
            return m_in.at[l]
        w = (f_in, g_in)[p]
        return w.at[l] if far(l) else w.at[l, 1]

    def slot(l, p, s):
        if p == 2:
            return mw.at[l, s]
        w = (fw, gw)[p]
        return w.at[l, :, s] if far(l) else w.at[l, 1, s]

    def w_copy(l, p, s, to, send, own):
        return pltpu.make_async_remote_copy(
            src_ref=own_block(l, p) if own else slot(l, p, s),
            dst_ref=slot(l, p, s),
            send_sem=send,
            recv_sem=w_recv.at[l * 3 + p, s],
            device_id={"tm": to},
            device_id_type=MESH,
        )

    def w_out(l, p, q):
        if q == 0:
            return w_copy(l, p, m, partner, w_send.at[l * 3 + p, 0], True)
        return w_copy(l, p, m, mate(q), w_send.at[l * 3 + p, q], True)

    def w_on(l, p, q):
        return w_copy(l, p, mate(q), partner, w_fwd.at[l * 3 + p, q], False)

    def w_mine(l, p):
        return pltpu.make_async_copy(own_block(l, p), slot(l, p, m), w_own.at[l * 3 + p])

    def w_start(l):
        for p in range(3):
            for q in others + [0]:
                w_out(l, p, q).start()
            w_mine(l, p).start()

    def w_forward(l, kinds):
        for p in kinds:
            for q in others:
                w_on(l, p, q).wait_recv()
                w_on(l, p, q).start()

    def w_ready(l, kinds):
        for p in kinds:
            w_mine(l, p).wait()
            w_copy(l, p, partner, partner, w_fwd.at[l * 3 + p, 0], False).wait_recv()
            for q in others:
                s = mate(q, partner)
                w_copy(l, p, s, partner, w_fwd.at[l * 3 + p, 0], False).wait_recv()

    def ag(i, src, buf, l, r, owner):
        return pltpu.make_async_remote_copy(
            src_ref=src,
            dst_ref=buf.at[l, owner],
            send_sem=ag_send.at[i, r],
            recv_sem=ag_recv.at[i, owner],
            device_id={"chan": peer(r)},
            device_id_type=MESH,
        )

    def ag_start(i, src, buf, l):
        for r in reversed(peers):
            ag(i, src, buf, l, r, c).start()

    def ag_wait(i, buf, l, r):
        ag(i, buf.at[l, c], buf, l, r, peer(r)).wait_recv()

    def rs(i, r, owner):
        return pltpu.make_async_remote_copy(
            src_ref=rsb.at[i, r],
            dst_ref=rsr.at[i, owner],
            send_sem=rs_send.at[i, r],
            recv_sem=rs_recv.at[i, owner],
            device_id={"chan": peer(r)},
            device_id_type=MESH,
        )

    def dl(l, hh, j):
        n = l * H + hh
        return pltpu.make_async_remote_copy(
            src_ref=sig.at[n, j],
            dst_ref=dly.at[n, j],
            send_sem=d_send.at[n, j],
            recv_sem=d_recv.at[n, j],
            device_id={"tm": lax.rem(m + span(l), tm)},
            device_id_type=MESH,
        )

    def fr(l, hh, j):
        n = l * H + hh
        return pltpu.make_async_remote_copy(
            src_ref=farb.at[n, j],
            dst_ref=farr.at[n, j],
            send_sem=f_send.at[n, j],
            recv_sem=f_recv.at[n, j],
            device_id={"tm": lax.rem(m + tm - span(l), tm)},
            device_id_type=MESH,
        )

    def block(w, l, tap, j):
        return w[l, tap, pl.ds(j * ratio, ratio)].reshape(cb, cb)

    barrier = pltpu.get_barrier_semaphore()
    for s in range(1, tm):
        pl.semaphore_signal(barrier, inc=1, device_id={"tm": lax.rem(m + s, tm)}, device_id_type=MESH)
    for s in range(1, chan):
        pl.semaphore_signal(barrier, inc=1, device_id={"chan": peer(s)}, device_id_type=MESH)
    pl.semaphore_wait(barrier, tm - 1 + chan - 1)

    def part(hh):
        return pl.ds(hh * half, half)

    for hh in range(H):
        ag_start(hh, rec.at[part(hh)], sig, hh)
    w_start(0)
    for hh in range(H):
        sig[hh, c] = rec[hh * half:(hh + 1) * half]
        gr[(layers - 1) * H + hh, c] = cot[hh * half:(hh + 1) * half]
    for l in range(1, layers):
        w_start(l)
    for hh in range(H):
        ag_start(layers * H + hh, cot.at[part(hh)], gr, (layers - 1) * H + hh)

    def near_taps(l, hh):
        n = l * H + hh
        if far(l):
            @pl.when(m < tm - span(l))
            def _():
                dl(l, hh, c).start()
                for r in peers:
                    ag_wait(n, sig, n, r)
                    dl(l, hh, peer(r)).start()

            @pl.when(m >= tm - span(l))
            def _():
                for r in peers:
                    ag_wait(n, sig, n, r)
        if hh == 0:
            if l == 0:
                w_forward(0, (0, 1))
            w_ready(l, (0, 1))
        for r in [0] + peers:
            j = peer(r)
            if r and not far(l):
                ag_wait(n, sig, n, r)
            x = sig[n, j]
            a = dot(x, block(fw, l, 1, j))
            b = dot(x, block(gw, l, 1, j))
            if r == 0:
                acc_f[hh] = a
                acc_g[hh] = b
            else:
                acc_f[hh] += a
                acc_g[hh] += b

    def mix_out(l, hh):
        n = l * H + hh
        if far(l):
            @pl.when(m >= span(l))
            def _():
                for r in [0] + peers:
                    j = peer(r)
                    dl(l, hh, j).wait_recv()
                    x = dly[n, j]
                    acc_f[hh] += dot(x, block(fw, l, 0, j))
                    acc_g[hh] += dot(x, block(gw, l, 0, j))
        th = jnp.tanh(acc_f[hh])
        sg = jax.nn.sigmoid(acc_g[hh])
        tval[n] = th
        sval[n] = sg
        gated = (th * sg).astype(BF)
        if hh == 0:
            if l == 0:
                w_forward(0, (2,))
            w_ready(l, (2,))

        def mixed(j):
            parts = [dot(gated, mw[l, j * ratio + i]) for i in range(ratio)]
            return parts[0] if ratio == 1 else jnp.concatenate(parts, axis=1)

        for r in reversed(peers):
            rsb[n, r] = mixed(peer(r)).astype(BF)
            rs(n, r, c).start()
        acc_f[hh] = mixed(c) + sig[n, c].astype(F32)

    def next_signal(l, hh):
        n = l * H + hh
        total = acc_f[hh]
        for r in peers:
            rs(n, r, peer(r)).wait_recv()
            total += rsr[n, peer(r)].astype(F32)
        if l + 1 < layers:
            sig[n + H, c] = total.astype(BF)
            ag_start(n + H, sig.at[n + H, c], sig, n + H)
        else:
            out[hh * half:(hh + 1) * half] = total.astype(BF)

    def run(l, first, second):
        if far(l):
            for hh in range(H):
                first(l, hh)
            for hh in range(H):
                second(l, hh)
        else:
            for hh in range(H):
                first(l, hh)
                second(l, hh)

    for l in range(layers):
        run(l, near_taps, mix_out)
        if l + 1 < layers:
            w_forward(l + 1, (0, 1, 2))
        for hh in range(H):
            next_signal(l, hh)

    order = list(reversed(peers)) + [0]

    def grads(l, hh):
        n = l * H + hh
        i = (2 * layers - 1 - l) * H + hh
        for r in [0] + peers:
            j = peer(r)
            if r:
                ag_wait(i, gr, n, r)
            g = gr[n, j]
            for k in range(ratio):
                z = dot_t(g[:, k * ob:(k + 1) * ob], mw[l, j * ratio + k])
                if r == 0 and k == 0:
                    acc_f[hh] = z
                else:
                    acc_f[hh] += z
        gz = acc_f[hh]
        th = tval[n]
        sg = sval[n]
        gf = (gz * sg * (1.0 - th * th)).astype(BF)
        gg = (gz * th * sg * (1.0 - sg)).astype(BF)
        gf_s[hh] = gf
        gg_s[hh] = gg
        if far(l):
            @pl.when(m >= span(l))
            def _():
                for r in order:
                    j = peer(r)
                    farb[n, j] = (dot_t(gf, block(fw, l, 0, j)) + dot_t(gg, block(gw, l, 0, j))).astype(BF)
                    fr(l, hh, j).start()

    def sums_out(l, hh):
        n = l * H + hh
        i = (2 * layers - 1 - l) * H + hh
        gf = gf_s[hh]
        gg = gg_s[hh]
        for r in order:
            j = peer(r)
            acc_g[hh] = dot_t(gf, block(fw, l, 1, j)) + dot_t(gg, block(gw, l, 1, j))
            if far(l):
                @pl.when(m < tm - span(l))
                def _():
                    fr(l, hh, j).wait_recv()
                    acc_g[hh] += farr[n, j].astype(F32)
            if r:
                rsb[i, r] = acc_g[hh].astype(BF)
                rs(i, r, c).start()
        acc_f[hh] = acc_g[hh] + gr[n, c].astype(F32)

    def next_grad(l, hh):
        n = l * H + hh
        i = (2 * layers - 1 - l) * H + hh
        total = acc_f[hh]
        for r in peers:
            rs(i, r, peer(r)).wait_recv()
            total += rsr[i, peer(r)].astype(F32)
        if l > 0:
            gr[n - H, c] = total.astype(BF)
            ag_start(i + H, gr.at[n - H, c], gr, n - H)
        else:
            gin[hh * half:(hh + 1) * half] = total.astype(BF)

    for l in reversed(range(layers)):
        run(l, grads, sums_out)
        for hh in range(H):
            next_grad(l, hh)

    for l in range(layers):
        for p in range(3):
            for q in others:
                w_out(l, p, q).wait_send()
                w_on(l, p, q).wait_send()
            w_out(l, p, 0).wait_send()
        if far(l):
            @pl.when(m < tm - span(l))
            def _():
                for hh in range(H):
                    for j in range(chan):
                        dl(l, hh, j).wait_send()

            @pl.when(m >= span(l))
            def _():
                for hh in range(H):
                    for j in range(chan):
                        fr(l, hh, j).wait_send()
    for i in range(2 * layers * H):
        for r in peers:
            ag(i, sig.at[0, c], sig, 0, r, c).wait_send()
            rs(i, r, c).wait_send()


def local(records, cotangent, filter_weight, gate_weight, mix_weight):
    tm, chan = lax.axis_size("tm"), lax.axis_size("chan")
    layers, taps, ib, cb = filter_weight.shape
    ob = mix_weight.shape[2]
    rows = records.shape[0]
    vmem = pl.BlockSpec(memory_space=pltpu.VMEM)
    hbm = pl.BlockSpec(memory_space=pl.ANY)
    weights = pltpu.VMEM((layers, taps, tm, ib, cb), BF)
    per_layer = pltpu.VMEM((H * layers, chan, rows // H, cb), BF)
    both = pltpu.VMEM((2 * H * layers, chan, rows // H, cb), BF)
    return pl.pallas_call(
        functools.partial(kernel, layers, tm, chan),
        out_shape=[jax.ShapeDtypeStruct(records.shape, BF)] * 2,
        in_specs=[vmem, vmem, hbm, hbm, hbm],
        out_specs=[vmem, vmem],
        scratch_shapes=[
            weights,
            weights,
            pltpu.VMEM((layers, tm, cb, ob), BF),
            per_layer,
            per_layer,
            both,
            both,
            per_layer,
            per_layer,
            per_layer,
            pltpu.VMEM((H * layers, rows // H, cb), F32),
            pltpu.VMEM((H * layers, rows // H, cb), F32),
            pltpu.VMEM((H, rows // H, cb), F32),
            pltpu.VMEM((H, rows // H, cb), F32),
            pltpu.VMEM((H, rows // H, cb), BF),
            pltpu.VMEM((H, rows // H, cb), BF),
            DMA((3 * layers, tm)),
            DMA((3 * layers, tm)),
            DMA((3 * layers, tm)),
            DMA((3 * layers,)),
            DMA((2 * H * layers, chan)),
            DMA((2 * H * layers, chan)),
            DMA((H * layers, chan)),
            DMA((H * layers, chan)),
            DMA((2 * H * layers, chan)),
            DMA((2 * H * layers, chan)),
            DMA((H * layers, chan)),
            DMA((H * layers, chan)),
        ],
        compiler_params=pltpu.CompilerParams(
            collective_id=0, has_side_effects=True, vmem_limit_bytes=56 * 2**20
        ),
    )(records, cotangent, filter_weight, gate_weight, mix_weight)


def solution(mesh):
    return jax.shard_map(
        local,
        mesh=mesh,
        in_specs=(
            P(("groups", "tm"), "chan"),
            P(("groups", "tm"), "chan"),
            P(None, None, "tm", "chan"),
            P(None, None, "tm", "chan"),
            P(None, "chan", "tm"),
        ),
        out_specs=(P(("groups", "tm"), "chan"), P(("groups", "tm"), "chan")),
        check_vma=False,
    )
```

```python
import functools

import jax
import jax.numpy as jnp
from jax import lax
from jax.experimental import pallas as pl
from jax.experimental.pallas import tpu as pltpu
from jax.sharding import PartitionSpec as P

MESH = pl.DeviceIdType.MESH
DMA = pltpu.SemaphoreType.DMA
BF = jnp.bfloat16
F32 = jnp.float32
H = 2


def dot(a, b):
    return jnp.dot(a, b, preferred_element_type=F32)


def dot_t(a, b):
    return lax.dot_general(a, b, (((1,), (1,)), ((), ())), preferred_element_type=F32)


def near_first(count):
    order = []
    for step in range(1, count // 2 + 1):
        for offset in (step, count - step):
            if offset not in order and offset < count:
                order.append(offset)
    return order


def kernel(
    layers, tm, chan,
    rec, cot, f_in, g_in, m_in,
    out, gin,
    fw, gw, mw, sig, dly, rsb, rsr, gr, farb, farr, tval, sval, acc_f, acc_g, gf_s, gg_s,
    w_send, w_recv, w_fwd, w_own,
    ag_send, ag_recv, d_send, d_recv, rs_send, rs_recv, f_send, f_recv,
):
    m = lax.axis_index("tm")
    c = lax.axis_index("chan")
    ratio = tm // chan
    rows, cb = rec.shape
    ob = mw.shape[-1]
    half = rows // H
    partner = m + 1 - 2 * lax.rem(m, 2)
    peers = near_first(chan)
    others = list(range(1, tm // 2))

    def peer(r):
        return lax.rem(c + r, chan)

    def mate(q, base=None):
        return lax.rem((m if base is None else base) + 2 * q, tm)

    def span(l):
        return 2**l

    def far(l):
        return span(l) < tm

    def own_block(l, p):
        if p == 2:
            return m_in.at[l]
        w = (f_in, g_in)[p]
        return w.at[l] if far(l) else w.at[l, 1]

    def slot(l, p, s):
        if p == 2:
            return mw.at[l, s]
        w = (fw, gw)[p]
        return w.at[l, :, s] if far(l) else w.at[l, 1, s]

    def w_copy(l, p, s, to, send, own):
        return pltpu.make_async_remote_copy(
            src_ref=own_block(l, p) if own else slot(l, p, s),
            dst_ref=slot(l, p, s),
            send_sem=send,
            recv_sem=w_recv.at[l * 3 + p, s],
            device_id={"tm": to},
            device_id_type=MESH,
        )

    def w_out(l, p, q):
        if q == 0:
            return w_copy(l, p, m, partner, w_send.at[l * 3 + p, 0], True)
        return w_copy(l, p, m, mate(q), w_send.at[l * 3 + p, q], True)

    def w_on(l, p, q):
        return w_copy(l, p, mate(q), partner, w_fwd.at[l * 3 + p, q], False)

    def w_mine(l, p):
        return pltpu.make_async_copy(own_block(l, p), slot(l, p, m), w_own.at[l * 3 + p])

    def w_start(l):
        for p in range(3):
            for q in others + [0]:
                w_out(l, p, q).start()
            w_mine(l, p).start()

    def w_forward(l, kinds):
        for p in kinds:
            for q in others:
                w_on(l, p, q).wait_recv()
                w_on(l, p, q).start()

    def w_ready(l, kinds):
        for p in kinds:
            w_mine(l, p).wait()
            w_copy(l, p, partner, partner, w_fwd.at[l * 3 + p, 0], False).wait_recv()
            for q in others:
                s = mate(q, partner)
                w_copy(l, p, s, partner, w_fwd.at[l * 3 + p, 0], False).wait_recv()

    def ag(i, src, buf, l, r, owner):
        return pltpu.make_async_remote_copy(
            src_ref=src,
            dst_ref=buf.at[l, owner],
            send_sem=ag_send.at[i, r],
            recv_sem=ag_recv.at[i, owner],
            device_id={"chan": peer(r)},
            device_id_type=MESH,
        )

    def ag_start(i, src, buf, l):
        for r in reversed(peers):
            ag(i, src, buf, l, r, c).start()

    def ag_wait(i, buf, l, r):
        ag(i, buf.at[l, c], buf, l, r, peer(r)).wait_recv()

    def rs(i, r, owner):
        return pltpu.make_async_remote_copy(
            src_ref=rsb.at[i, r],
            dst_ref=rsr.at[i, owner],
            send_sem=rs_send.at[i, r],
            recv_sem=rs_recv.at[i, owner],
            device_id={"chan": peer(r)},
            device_id_type=MESH,
        )

    def dl(l, hh, j):
        n = l * H + hh
        return pltpu.make_async_remote_copy(
            src_ref=sig.at[n, j],
            dst_ref=dly.at[n, j],
            send_sem=d_send.at[n, j],
            recv_sem=d_recv.at[n, j],
            device_id={"tm": lax.rem(m + span(l), tm)},
            device_id_type=MESH,
        )

    def fr(l, hh, j):
        n = l * H + hh
        return pltpu.make_async_remote_copy(
            src_ref=farb.at[n, j],
            dst_ref=farr.at[n, j],
            send_sem=f_send.at[n, j],
            recv_sem=f_recv.at[n, j],
            device_id={"tm": lax.rem(m + tm - span(l), tm)},
            device_id_type=MESH,
        )

    def block(w, l, tap, j):
        return w[l, tap, pl.ds(j * ratio, ratio)].reshape(cb, cb)

    barrier = pltpu.get_barrier_semaphore()
    for s in range(1, tm):
        pl.semaphore_signal(barrier, inc=1, device_id={"tm": lax.rem(m + s, tm)}, device_id_type=MESH)
    for s in range(1, chan):
        pl.semaphore_signal(barrier, inc=1, device_id={"chan": peer(s)}, device_id_type=MESH)
    pl.semaphore_wait(barrier, tm - 1 + chan - 1)

    def part(hh):
        return pl.ds(hh * half, half)

    for hh in range(H):
        ag_start(hh, rec.at[part(hh)], sig, hh)
    w_start(0)
    for hh in range(H):
        sig[hh, c] = rec[hh * half:(hh + 1) * half]
        gr[(layers - 1) * H + hh, c] = cot[hh * half:(hh + 1) * half]
    for hh in range(H):
        ag_start(layers * H + hh, cot.at[part(hh)], gr, (layers - 1) * H + hh)

    def near_taps(l, hh):
        n = l * H + hh
        if far(l):
            @pl.when(m < tm - span(l))
            def _():
                dl(l, hh, c).start()
                for r in peers:
                    ag_wait(n, sig, n, r)
                    dl(l, hh, peer(r)).start()

            @pl.when(m >= tm - span(l))
            def _():
                for r in peers:
                    ag_wait(n, sig, n, r)
        if hh == H - 1:
            for later in range(1, layers):
                if min(later - 1, 1) == l:
                    w_start(later)
        if hh == 0:
            if l == 0:
                w_forward(0, (0, 1))
            w_ready(l, (0, 1))
        for r in [0] + peers:
            j = peer(r)
            if r and not far(l):
                ag_wait(n, sig, n, r)
            x = sig[n, j]
            a = dot(x, block(fw, l, 1, j))
            b = dot(x, block(gw, l, 1, j))
            if r == 0:
                acc_f[hh] = a
                acc_g[hh] = b
            else:
                acc_f[hh] += a
                acc_g[hh] += b

    def mix_out(l, hh):
        n = l * H + hh
        if far(l):
            @pl.when(m >= span(l))
            def _():
                for r in [0] + peers:
                    j = peer(r)
                    dl(l, hh, j).wait_recv()
                    x = dly[n, j]
                    acc_f[hh] += dot(x, block(fw, l, 0, j))
                    acc_g[hh] += dot(x, block(gw, l, 0, j))
        th = jnp.tanh(acc_f[hh])
        sg = jax.nn.sigmoid(acc_g[hh])
        tval[n] = th
        sval[n] = sg
        gated = (th * sg).astype(BF)
        if hh == 0:
            if l == 0:
                w_forward(0, (2,))
            w_ready(l, (2,))

        def mixed(j):
            parts = [dot(gated, mw[l, j * ratio + i]) for i in range(ratio)]
            return parts[0] if ratio == 1 else jnp.concatenate(parts, axis=1)

        for r in reversed(peers):
            rsb[n, r] = mixed(peer(r)).astype(BF)
            rs(n, r, c).start()
        acc_f[hh] = mixed(c) + sig[n, c].astype(F32)

    def next_signal(l, hh):
        n = l * H + hh
        total = acc_f[hh]
        for r in peers:
            rs(n, r, peer(r)).wait_recv()
            total += rsr[n, peer(r)].astype(F32)
        if l + 1 < layers:
            sig[n + H, c] = total.astype(BF)
            ag_start(n + H, sig.at[n + H, c], sig, n + H)
        else:
            out[hh * half:(hh + 1) * half] = total.astype(BF)

    def run(l, first, second):
        if far(l):
            for hh in range(H):
                first(l, hh)
            for hh in range(H):
                second(l, hh)
        else:
            for hh in range(H):
                first(l, hh)
                second(l, hh)

    for l in range(layers):
        run(l, near_taps, mix_out)
        for hh in range(H):
            next_signal(l, hh)
        if l + 1 < layers:
            w_forward(l + 1, (0, 1, 2))

    order = list(reversed(peers)) + [0]

    def grads(l, hh):
        n = l * H + hh
        i = (2 * layers - 1 - l) * H + hh
        for r in [0] + peers:
            j = peer(r)
            if r:
                ag_wait(i, gr, n, r)
            g = gr[n, j]
            for k in range(ratio):
                z = dot_t(g[:, k * ob:(k + 1) * ob], mw[l, j * ratio + k])
                if r == 0 and k == 0:
                    acc_f[hh] = z
                else:
                    acc_f[hh] += z
        gz = acc_f[hh]
        th = tval[n]
        sg = sval[n]
        gf = (gz * sg * (1.0 - th * th)).astype(BF)
        gg = (gz * th * sg * (1.0 - sg)).astype(BF)
        gf_s[hh] = gf
        gg_s[hh] = gg
        if far(l):
            @pl.when(m >= span(l))
            def _():
                for r in order:
                    j = peer(r)
                    farb[n, j] = (dot_t(gf, block(fw, l, 0, j)) + dot_t(gg, block(gw, l, 0, j))).astype(BF)
                    fr(l, hh, j).start()

    def sums_out(l, hh):
        n = l * H + hh
        i = (2 * layers - 1 - l) * H + hh
        gf = gf_s[hh]
        gg = gg_s[hh]
        for r in order:
            j = peer(r)
            acc_g[hh] = dot_t(gf, block(fw, l, 1, j)) + dot_t(gg, block(gw, l, 1, j))
            if far(l):
                @pl.when(m < tm - span(l))
                def _():
                    fr(l, hh, j).wait_recv()
                    acc_g[hh] += farr[n, j].astype(F32)
            if r:
                rsb[i, r] = acc_g[hh].astype(BF)
                rs(i, r, c).start()
        acc_f[hh] = acc_g[hh] + gr[n, c].astype(F32)

    def next_grad(l, hh):
        n = l * H + hh
        i = (2 * layers - 1 - l) * H + hh
        total = acc_f[hh]
        for r in peers:
            rs(i, r, peer(r)).wait_recv()
            total += rsr[i, peer(r)].astype(F32)
        if l > 0:
            gr[n - H, c] = total.astype(BF)
            ag_start(i + H, gr.at[n - H, c], gr, n - H)
        else:
            gin[hh * half:(hh + 1) * half] = total.astype(BF)

    for l in reversed(range(layers)):
        run(l, grads, sums_out)
        for hh in range(H):
            next_grad(l, hh)

    for l in range(layers):
        for p in range(3):
            for q in others:
                w_out(l, p, q).wait_send()
                w_on(l, p, q).wait_send()
            w_out(l, p, 0).wait_send()
        if far(l):
            @pl.when(m < tm - span(l))
            def _():
                for hh in range(H):
                    for j in range(chan):
                        dl(l, hh, j).wait_send()

            @pl.when(m >= span(l))
            def _():
                for hh in range(H):
                    for j in range(chan):
                        fr(l, hh, j).wait_send()
    for i in range(2 * layers * H):
        for r in peers:
            ag(i, sig.at[0, c], sig, 0, r, c).wait_send()
            rs(i, r, c).wait_send()


def local(records, cotangent, filter_weight, gate_weight, mix_weight):
    tm, chan = lax.axis_size("tm"), lax.axis_size("chan")
    layers, taps, ib, cb = filter_weight.shape
    ob = mix_weight.shape[2]
    rows = records.shape[0]
    vmem = pl.BlockSpec(memory_space=pltpu.VMEM)
    hbm = pl.BlockSpec(memory_space=pl.ANY)
    weights = pltpu.VMEM((layers, taps, tm, ib, cb), BF)
    per_layer = pltpu.VMEM((H * layers, chan, rows // H, cb), BF)
    both = pltpu.VMEM((2 * H * layers, chan, rows // H, cb), BF)
    return pl.pallas_call(
        functools.partial(kernel, layers, tm, chan),
        out_shape=[jax.ShapeDtypeStruct(records.shape, BF)] * 2,
        in_specs=[vmem, vmem, hbm, hbm, hbm],
        out_specs=[vmem, vmem],
        scratch_shapes=[
            weights,
            weights,
            pltpu.VMEM((layers, tm, cb, ob), BF),
            per_layer,
            per_layer,
            both,
            both,
            per_layer,
            per_layer,
            per_layer,
            pltpu.VMEM((H * layers, rows // H, cb), F32),
            pltpu.VMEM((H * layers, rows // H, cb), F32),
            pltpu.VMEM((H, rows // H, cb), F32),
            pltpu.VMEM((H, rows // H, cb), F32),
            pltpu.VMEM((H, rows // H, cb), BF),
            pltpu.VMEM((H, rows // H, cb), BF),
            DMA((3 * layers, tm)),
            DMA((3 * layers, tm)),
            DMA((3 * layers, tm)),
            DMA((3 * layers,)),
            DMA((2 * H * layers, chan)),
            DMA((2 * H * layers, chan)),
            DMA((H * layers, chan)),
            DMA((H * layers, chan)),
            DMA((2 * H * layers, chan)),
            DMA((2 * H * layers, chan)),
            DMA((H * layers, chan)),
            DMA((H * layers, chan)),
        ],
        compiler_params=pltpu.CompilerParams(
            collective_id=0, has_side_effects=True, vmem_limit_bytes=56 * 2**20
        ),
    )(records, cotangent, filter_weight, gate_weight, mix_weight)


def solution(mesh):
    return jax.shard_map(
        local,
        mesh=mesh,
        in_specs=(
            P(("groups", "tm"), "chan"),
            P(("groups", "tm"), "chan"),
            P(None, None, "tm", "chan"),
            P(None, None, "tm", "chan"),
            P(None, "chan", "tm"),
        ),
        out_specs=(P(("groups", "tm"), "chan"), P(("groups", "tm"), "chan")),
        check_vma=False,
    )
```

```python
import functools

import jax
import jax.numpy as jnp
from jax import lax
from jax.experimental import pallas as pl
from jax.experimental.pallas import tpu as pltpu
from jax.sharding import PartitionSpec as P

MESH = pl.DeviceIdType.MESH
DMA = pltpu.SemaphoreType.DMA
BF = jnp.bfloat16
F32 = jnp.float32
H = 2


def dot(a, b):
    return jnp.dot(a, b, preferred_element_type=F32)


def dot_t(a, b):
    return lax.dot_general(a, b, (((1,), (1,)), ((), ())), preferred_element_type=F32)


def near_first(count):
    order = []
    for step in range(1, count // 2 + 1):
        for offset in (step, count - step):
            if offset not in order and offset < count:
                order.append(offset)
    return order


def kernel(
    layers, tm, chan,
    rec, cot, f_in, g_in, m_in,
    out, gin,
    fw, gw, mw, sig, dly, rsb, rsr, gr, farb, farr, tval, sval, acc_f, acc_g, gf_s, gg_s,
    w_send, w_recv, w_fwd, w_own,
    ag_send, ag_fwd, ag_recv, d_send, d_recv, rs_send, rs_recv, f_send, f_recv,
):
    m = lax.axis_index("tm")
    c = lax.axis_index("chan")
    ratio = tm // chan
    rows, cb = rec.shape
    ob = mw.shape[-1]
    half = rows // H
    partner = m + 1 - 2 * lax.rem(m, 2)
    peers = near_first(chan)
    others = list(range(1, tm // 2))
    seconds = list(range(1, chan // 2))
    pair = c + 1 - 2 * lax.rem(c, 2)

    def peer(r):
        return lax.rem(c + r, chan)

    def mate(q, base=None):
        return lax.rem((m if base is None else base) + 2 * q, tm)

    def span(l):
        return 2**l

    def far(l):
        return span(l) < tm

    def own_block(l, p):
        if p == 2:
            return m_in.at[l]
        w = (f_in, g_in)[p]
        return w.at[l] if far(l) else w.at[l, 1]

    def slot(l, p, s):
        if p == 2:
            return mw.at[l, s]
        w = (fw, gw)[p]
        return w.at[l, :, s] if far(l) else w.at[l, 1, s]

    def w_copy(l, p, s, to, send, own):
        return pltpu.make_async_remote_copy(
            src_ref=own_block(l, p) if own else slot(l, p, s),
            dst_ref=slot(l, p, s),
            send_sem=send,
            recv_sem=w_recv.at[l * 3 + p, s],
            device_id={"tm": to},
            device_id_type=MESH,
        )

    def w_out(l, p, q):
        if q == 0:
            return w_copy(l, p, m, partner, w_send.at[l * 3 + p, 0], True)
        return w_copy(l, p, m, mate(q), w_send.at[l * 3 + p, q], True)

    def w_on(l, p, q):
        return w_copy(l, p, mate(q), partner, w_fwd.at[l * 3 + p, q], False)

    def w_mine(l, p):
        return pltpu.make_async_copy(own_block(l, p), slot(l, p, m), w_own.at[l * 3 + p])

    def w_start(l):
        for p in range(3):
            for q in others + [0]:
                w_out(l, p, q).start()
            w_mine(l, p).start()

    def w_forward(l, kinds):
        for p in kinds:
            for q in others:
                w_on(l, p, q).wait_recv()
                w_on(l, p, q).start()

    def w_ready(l, kinds):
        for p in kinds:
            w_mine(l, p).wait()
            w_copy(l, p, partner, partner, w_fwd.at[l * 3 + p, 0], False).wait_recv()
            for q in others:
                s = mate(q, partner)
                w_copy(l, p, s, partner, w_fwd.at[l * 3 + p, 0], False).wait_recv()

    def ag(i, src, buf, l, to, owner, send):
        return pltpu.make_async_remote_copy(
            src_ref=src,
            dst_ref=buf.at[l, owner],
            send_sem=send,
            recv_sem=ag_recv.at[i, owner],
            device_id={"chan": to},
            device_id_type=MESH,
        )

    def ag_out(i, src, buf, l, q):
        return ag(i, src, buf, l, peer(2 * q) if q else pair, c, ag_send.at[i, q])

    def ag_on(i, buf, l, q):
        return ag(i, buf.at[l, peer(2 * q)], buf, l, pair, peer(2 * q), ag_fwd.at[i, q])

    def ag_start(i, src, buf, l):
        for q in seconds + [0]:
            ag_out(i, src, buf, l, q).start()

    def ag_relay(i, buf, l):
        for q in seconds:
            ag_on(i, buf, l, q).wait_recv()
            ag_on(i, buf, l, q).start()

    def ag_wait(i, buf, l, j):
        ag(i, buf.at[l, c], buf, l, pair, j, ag_send.at[i, 0]).wait_recv()

    def here():
        return [c] + [peer(2 * q) for q in seconds]

    def coming():
        return [pair] + [lax.rem(pair + 2 * q, chan) for q in seconds]

    def rs(i, r, owner):
        return pltpu.make_async_remote_copy(
            src_ref=rsb.at[i, r],
            dst_ref=rsr.at[i, owner],
            send_sem=rs_send.at[i, r],
            recv_sem=rs_recv.at[i, owner],
            device_id={"chan": peer(r)},
            device_id_type=MESH,
        )

    def dl(l, hh, j):
        n = l * H + hh
        return pltpu.make_async_remote_copy(
            src_ref=sig.at[n, j],
            dst_ref=dly.at[n, j],
            send_sem=d_send.at[n, j],
            recv_sem=d_recv.at[n, j],
            device_id={"tm": lax.rem(m + span(l), tm)},
            device_id_type=MESH,
        )

    def fr(l, hh, j):
        n = l * H + hh
        return pltpu.make_async_remote_copy(
            src_ref=farb.at[n, j],
            dst_ref=farr.at[n, j],
            send_sem=f_send.at[n, j],
            recv_sem=f_recv.at[n, j],
            device_id={"tm": lax.rem(m + tm - span(l), tm)},
            device_id_type=MESH,
        )

    def block(w, l, tap, j):
        return w[l, tap, pl.ds(j * ratio, ratio)].reshape(cb, cb)

    barrier = pltpu.get_barrier_semaphore()
    for s in range(1, tm):
        pl.semaphore_signal(barrier, inc=1, device_id={"tm": lax.rem(m + s, tm)}, device_id_type=MESH)
    for s in range(1, chan):
        pl.semaphore_signal(barrier, inc=1, device_id={"chan": peer(s)}, device_id_type=MESH)
    pl.semaphore_wait(barrier, tm - 1 + chan - 1)

    def part(hh):
        return pl.ds(hh * half, half)

    for hh in range(H):
        ag_start(hh, rec.at[part(hh)], sig, hh)
    w_start(0)
    for hh in range(H):
        sig[hh, c] = rec[hh * half:(hh + 1) * half]
        gr[(layers - 1) * H + hh, c] = cot[hh * half:(hh + 1) * half]
    for hh in range(H):
        ag_start(layers * H + hh, cot.at[part(hh)], gr, (layers - 1) * H + hh)

    def near_taps(l, hh):
        n = l * H + hh
        if far(l):
            @pl.when(m < tm - span(l))
            def _():
                for j in here():
                    dl(l, hh, j).start()
                for j in coming():
                    ag_wait(n, sig, n, j)
                    dl(l, hh, j).start()

            @pl.when(m >= tm - span(l))
            def _():
                for j in coming():
                    ag_wait(n, sig, n, j)
        if hh == H - 1:
            for later in range(1, layers):
                if min(later - 1, 1) == l:
                    w_start(later)
        if hh == 0:
            if l == 0:
                w_forward(0, (0, 1))
            w_ready(l, (0, 1))
        for r, j in enumerate(here() + coming()):
            if r >= chan // 2 and not far(l):
                ag_wait(n, sig, n, j)
            x = sig[n, j]
            a = dot(x, block(fw, l, 1, j))
            b = dot(x, block(gw, l, 1, j))
            if r == 0:
                acc_f[hh] = a
                acc_g[hh] = b
            else:
                acc_f[hh] += a
                acc_g[hh] += b

    def mix_out(l, hh):
        n = l * H + hh
        if far(l):
            @pl.when(m >= span(l))
            def _():
                for j in here() + coming():
                    dl(l, hh, j).wait_recv()
                    x = dly[n, j]
                    acc_f[hh] += dot(x, block(fw, l, 0, j))
                    acc_g[hh] += dot(x, block(gw, l, 0, j))
        th = jnp.tanh(acc_f[hh])
        sg = jax.nn.sigmoid(acc_g[hh])
        tval[n] = th
        sval[n] = sg
        gated = (th * sg).astype(BF)
        if hh == 0:
            if l == 0:
                w_forward(0, (2,))
            w_ready(l, (2,))

        def mixed(j):
            parts = [dot(gated, mw[l, j * ratio + i]) for i in range(ratio)]
            return parts[0] if ratio == 1 else jnp.concatenate(parts, axis=1)

        for r in reversed(peers):
            rsb[n, r] = mixed(peer(r)).astype(BF)
            rs(n, r, c).start()
        acc_f[hh] = mixed(c) + sig[n, c].astype(F32)

    def next_signal(l, hh):
        n = l * H + hh
        total = acc_f[hh]
        for r in peers:
            rs(n, r, peer(r)).wait_recv()
            total += rsr[n, peer(r)].astype(F32)
        if l + 1 < layers:
            sig[n + H, c] = total.astype(BF)
            ag_start(n + H, sig.at[n + H, c], sig, n + H)
        else:
            out[hh * half:(hh + 1) * half] = total.astype(BF)

    def run(l, first, second):
        if far(l):
            for hh in range(H):
                first(l, hh)
            for hh in range(H):
                second(l, hh)
        else:
            for hh in range(H):
                first(l, hh)
                second(l, hh)

    for l in range(layers):
        for hh in range(H):
            ag_relay(l * H + hh, sig, l * H + hh)
        if l == 1 or layers == 1:
            for hh in range(H):
                ag_relay(layers * H + hh, gr, (layers - 1) * H + hh)
        run(l, near_taps, mix_out)
        for hh in range(H):
            next_signal(l, hh)
        if l + 1 < layers:
            w_forward(l + 1, (0, 1, 2))

    order = list(reversed(peers)) + [0]

    def grads(l, hh):
        n = l * H + hh
        i = (2 * layers - 1 - l) * H + hh
        for r, j in enumerate(here() + coming()):
            if r >= chan // 2:
                ag_wait(i, gr, n, j)
            g = gr[n, j]
            for k in range(ratio):
                z = dot_t(g[:, k * ob:(k + 1) * ob], mw[l, j * ratio + k])
                if r == 0 and k == 0:
                    acc_f[hh] = z
                else:
                    acc_f[hh] += z
        gz = acc_f[hh]
        th = tval[n]
        sg = sval[n]
        gf = (gz * sg * (1.0 - th * th)).astype(BF)
        gg = (gz * th * sg * (1.0 - sg)).astype(BF)
        gf_s[hh] = gf
        gg_s[hh] = gg
        if far(l):
            @pl.when(m >= span(l))
            def _():
                for r in order:
                    j = peer(r)
                    farb[n, j] = (dot_t(gf, block(fw, l, 0, j)) + dot_t(gg, block(gw, l, 0, j))).astype(BF)
                    fr(l, hh, j).start()

    def sums_out(l, hh):
        n = l * H + hh
        i = (2 * layers - 1 - l) * H + hh
        gf = gf_s[hh]
        gg = gg_s[hh]
        for r in order:
            j = peer(r)
            acc_g[hh] = dot_t(gf, block(fw, l, 1, j)) + dot_t(gg, block(gw, l, 1, j))
            if far(l):
                @pl.when(m < tm - span(l))
                def _():
                    fr(l, hh, j).wait_recv()
                    acc_g[hh] += farr[n, j].astype(F32)
            if r:
                rsb[i, r] = acc_g[hh].astype(BF)
                rs(i, r, c).start()
        acc_f[hh] = acc_g[hh] + gr[n, c].astype(F32)

    def next_grad(l, hh):
        n = l * H + hh
        i = (2 * layers - 1 - l) * H + hh
        total = acc_f[hh]
        for r in peers:
            rs(i, r, peer(r)).wait_recv()
            total += rsr[i, peer(r)].astype(F32)
        if l > 0:
            gr[n - H, c] = total.astype(BF)
            ag_start(i + H, gr.at[n - H, c], gr, n - H)
        else:
            gin[hh * half:(hh + 1) * half] = total.astype(BF)

    for l in reversed(range(layers)):
        if l < layers - 1:
            for hh in range(H):
                ag_relay((2 * layers - 1 - l) * H + hh, gr, l * H + hh)
        run(l, grads, sums_out)
        for hh in range(H):
            next_grad(l, hh)

    for l in range(layers):
        for p in range(3):
            for q in others:
                w_out(l, p, q).wait_send()
                w_on(l, p, q).wait_send()
            w_out(l, p, 0).wait_send()
        if far(l):
            @pl.when(m < tm - span(l))
            def _():
                for hh in range(H):
                    for j in range(chan):
                        dl(l, hh, j).wait_send()

            @pl.when(m >= span(l))
            def _():
                for hh in range(H):
                    for j in range(chan):
                        fr(l, hh, j).wait_send()
    for i in range(2 * layers * H):
        for q in seconds:
            ag_on(i, sig, 0, q).wait_send()
        for q in [0] + seconds:
            ag_out(i, sig.at[0, c], sig, 0, q).wait_send()
        for r in peers:
            rs(i, r, c).wait_send()


def local(records, cotangent, filter_weight, gate_weight, mix_weight):
    tm, chan = lax.axis_size("tm"), lax.axis_size("chan")
    layers, taps, ib, cb = filter_weight.shape
    ob = mix_weight.shape[2]
    rows = records.shape[0]
    vmem = pl.BlockSpec(memory_space=pltpu.VMEM)
    hbm = pl.BlockSpec(memory_space=pl.ANY)
    weights = pltpu.VMEM((layers, taps, tm, ib, cb), BF)
    per_layer = pltpu.VMEM((H * layers, chan, rows // H, cb), BF)
    both = pltpu.VMEM((2 * H * layers, chan, rows // H, cb), BF)
    return pl.pallas_call(
        functools.partial(kernel, layers, tm, chan),
        out_shape=[jax.ShapeDtypeStruct(records.shape, BF)] * 2,
        in_specs=[vmem, vmem, hbm, hbm, hbm],
        out_specs=[vmem, vmem],
        scratch_shapes=[
            weights,
            weights,
            pltpu.VMEM((layers, tm, cb, ob), BF),
            per_layer,
            per_layer,
            both,
            both,
            per_layer,
            per_layer,
            per_layer,
            pltpu.VMEM((H * layers, rows // H, cb), F32),
            pltpu.VMEM((H * layers, rows // H, cb), F32),
            pltpu.VMEM((H, rows // H, cb), F32),
            pltpu.VMEM((H, rows // H, cb), F32),
            pltpu.VMEM((H, rows // H, cb), BF),
            pltpu.VMEM((H, rows // H, cb), BF),
            DMA((3 * layers, tm)),
            DMA((3 * layers, tm)),
            DMA((3 * layers, tm)),
            DMA((3 * layers,)),
            DMA((2 * H * layers, chan)),
            DMA((2 * H * layers, chan)),
            DMA((2 * H * layers, chan)),
            DMA((H * layers, chan)),
            DMA((H * layers, chan)),
            DMA((2 * H * layers, chan)),
            DMA((2 * H * layers, chan)),
            DMA((H * layers, chan)),
            DMA((H * layers, chan)),
        ],
        compiler_params=pltpu.CompilerParams(
            collective_id=0, has_side_effects=True, vmem_limit_bytes=56 * 2**20
        ),
    )(records, cotangent, filter_weight, gate_weight, mix_weight)


def solution(mesh):
    return jax.shard_map(
        local,
        mesh=mesh,
        in_specs=(
            P(("groups", "tm"), "chan"),
            P(("groups", "tm"), "chan"),
            P(None, None, "tm", "chan"),
            P(None, None, "tm", "chan"),
            P(None, "chan", "tm"),
        ),
        out_specs=(P(("groups", "tm"), "chan"), P(("groups", "tm"), "chan")),
        check_vma=False,
    )
```
